32 devices in a mesh: region: 4 (over y, core), member: 8 (over z, x).
Axes of the slice: x: 2, y: 2, z: 4, core: 2. Of those that a mesh axis runs over, the one named last changes fastest.
Arguments:
- initial_ensemble: float32 [256, 32768], P('member', 'region'), may hold values from -18 to 18
- driving_term: float32 [32768], P('region'), may hold values from 4 to 12
- observation_cells: int32 [1, 2, 64, 128], P(None, None, ('region', 'member')), may hold values from 0 to 1023
- observation_values: float32 [1, 2, 64, 128], P(None, None, ('region', 'member')), may hold values from -12 to 12
- observation_weight: float32 [1, 2, 64, 128], P(None, None, ('region', 'member')), may hold values from 0.25 to 4
- block_tile_list: int32 [1, 2, 64, 4], P(None, None, ('region', 'member')), may hold values from 0 to 63, as said below
- block_tile_count: int32 [1, 2, 64], P(None, None, ('region', 'member')), may hold values from 1 to 4, as said below
Outputs:
- analysis: float32 [256, 32768], P('member', 'region')
The draws below stay inside these ranges and needn't reach their ends.
Inputs may be any that keep to these rules, and one draw needn't show every extreme that they name: For s < block_tile_count[c, p, b] the entries block_tile_list[c, p, b, s] are distinct tiles whose owner t // 2 is b // 2 - 1, b // 2 or b // 2 + 1, taken modulo 64 // 2; entries at s >= block_tile_count[c, p, b] are ignored. `block_tile_count`: in every cycle and pass some block lists 4 tiles.
All inputs are finite; a program needn't handle non-finite values.
Results may differ from the reference program's by a relative error of at most 0.0003.
Values sent between devices are 32-bit elements; how exact they have to be, the bound alone decides.
A program may use at most 64 MiB of HBM per device.

```python
import math
import jax
import jax.numpy as jnp
from jax import lax

ENSEMBLE_SIZE = 256
CELLS_DEV = 1024
BLOCK = 512
TILE = 128
PATCHES_PER_UNIT = 2
L_MAX = 4
NS_ITERS = 10
STEPS = 4
PASSES = 2
CYCLES = 1
BLK_DEV = 2
GRID_CELLS = 32768
NBLK = 64
NTILES = 64


def draw_block_tile_list(key, part):
    base_key = jax.random.fold_in(key, 11)
    row_count = CYCLES * PASSES * NBLK
    nearby = 3 * PATCHES_PER_UNIT
    ranking_marks = jax.random.randint(base_key, (row_count, nearby), 0, 1 << 20) * nearby + jnp.arange(nearby, dtype=jnp.int32)[None, :]
    ranked = jnp.argsort(ranking_marks, axis=1, stable=True)[:, :L_MAX].astype(jnp.int32)
    blocks = jnp.tile(jnp.arange(NBLK, dtype=jnp.int32), CYCLES * PASSES)
    owners = blocks // BLK_DEV - 1
    tile_ids = (owners[:, None] * PATCHES_PER_UNIT + ranked) % NTILES
    return tile_ids.reshape(CYCLES, PASSES, NBLK, L_MAX).astype(jnp.int32)


def draw_block_tile_count(key, part):
    base_key = jax.random.fold_in(key, 23)
    first_key, second_key, third_key = jax.random.split(base_key, 3)
    lower = jnp.minimum(jax.random.randint(first_key, (CYCLES, PASSES, NBLK), 1, L_MAX + 1), jax.random.randint(second_key, (CYCLES, PASSES, NBLK), 1, L_MAX + 1))
    fullest = jax.random.randint(third_key, (CYCLES, PASSES, 1), 0, NBLK)
    placed = jnp.arange(NBLK, dtype=jnp.int32)[None, None, :] == fullest
    return jnp.where(placed, L_MAX, lower).astype(jnp.int32)


def with_ends(values, stream_key, least, largest):
    longest = values.shape.index(max(values.shape))
    spots = []
    for shift in (0, 1):
        where = [jax.random.randint(jax.random.fold_in(stream_key, axis), (), 0, length) for axis, length in enumerate(values.shape)]
        where[longest] = (where[longest] + shift) % values.shape[longest]
        spots.append(tuple(where))
    return values.at[spots[0]].set(least).at[spots[1]].set(largest)


def block_levels(stream_key, extent, cuts, low, largest):
    def one(position, parts):
        draws = jax.random.uniform(jax.random.fold_in(jax.random.fold_in(stream_key, 6), position), (parts,), jnp.float32, low / len(cuts), largest / len(cuts))
        return jnp.repeat(jnp.exp(draws), extent[position] // parts).reshape((-1,) + (1,) * (len(extent) - position - 1))

    factor_of = one(*cuts[0])
    for cut in cuts[1:]:
        factor_of = factor_of * one(*cut)
    return factor_of


def scatter_about(stream_key, dims, scale, bound, cuts=(), kind=jnp.bfloat16):
    level = block_levels(stream_key, dims, cuts, -0.22, 0.18) if cuts else 1.0
    drawn = jax.random.normal(stream_key, dims, jnp.float32) * scale * level
    return jnp.minimum(jnp.maximum(drawn, -bound), bound).astype(kind)


def setup_inputs(seed: int = 0) -> dict:
    key_list = jax.random.split(jax.random.key(seed), 8)
    return {
        "initial_ensemble": scatter_about(key_list[0], (ENSEMBLE_SIZE, GRID_CELLS), 3.0, 18.0, ((0, 8), (1, 4)), jnp.float32),
        "driving_term": jnp.clip(jnp.exp(math.log(12.0) - 1.0986123 * jax.random.uniform(key_list[1], (GRID_CELLS,), jnp.float32) ** block_levels(key_list[1], (GRID_CELLS,), ((0, 4),), -0.2, 0.2)), 4.0, 12.0),
        "observation_cells": with_ends(jax.random.randint(key_list[2], (CYCLES, PASSES, NTILES, TILE), 0, CELLS_DEV), jax.random.fold_in(key_list[2], 1), 0, CELLS_DEV - 1).astype(jnp.int32),
        "observation_values": scatter_about(key_list[3], (CYCLES, PASSES, NTILES, TILE), 2.0, 12.0, ((2, 32),), jnp.float32),
        "observation_weight": jnp.clip(jnp.exp(math.log(4.0) - 2.7725887 * jax.random.uniform(key_list[4], (CYCLES, PASSES, NTILES, TILE), jnp.float32) ** block_levels(key_list[4], (CYCLES, PASSES, NTILES, TILE), ((2, 32),), -0.2, 0.2)), 0.25, 4.0),
        "block_tile_list": draw_block_tile_list(jax.random.fold_in(key_list[7], 71), 0),
        "block_tile_count": draw_block_tile_count(jax.random.fold_in(key_list[7], 71), 0),
    }


time_step = 0.05
highest_precision = lax.Precision.HIGHEST

def background_prediction(replica_dynamics_vector, driving_term):
    for step_index in range(STEPS):
        ahead_one = jnp.roll(replica_dynamics_vector, -1, axis=1)
        further = jnp.roll(replica_dynamics_vector, 2, axis=1)
        behind = jnp.roll(replica_dynamics_vector, 1, axis=1)
        replica_dynamics_vector = replica_dynamics_vector + time_step * ((ahead_one - further) * behind - replica_dynamics_vector + driving_term)
    return replica_dynamics_vector

def ensemble_transform(gram, pulled):
    identity = jnp.eye(ENSEMBLE_SIZE, dtype=jnp.float32)
    system = gram + (ENSEMBLE_SIZE - 1) * identity
    frob_norm = jnp.sqrt(jnp.sum(system * system))
    root_iter = system / frob_norm
    inv_iter = identity
    for repeat_index in range(NS_ITERS):
        factor = 1.5 * identity - 0.5 * jnp.dot(inv_iter, root_iter, precision=highest_precision)
        root_iter = jnp.dot(root_iter, factor, precision=highest_precision)
        inv_iter = jnp.dot(factor, inv_iter, precision=highest_precision)
    inv_root = inv_iter / jnp.sqrt(frob_norm)
    mean_shift = jnp.dot(inv_root, jnp.dot(inv_root, pulled, precision=highest_precision), precision=highest_precision)
    return math.sqrt(ENSEMBLE_SIZE - 1) * inv_root + mean_shift[:, None]

def analyse_block(segment_readings, spreads, innovs):
    gram = jnp.einsum('lkp,ljp->kj', spreads, spreads, precision=highest_precision)
    pulled = jnp.einsum('lkp,lp->k', spreads, innovs, precision=highest_precision)
    transform = ensemble_transform(gram, pulled)
    center = lax.optimization_barrier(jnp.mean(segment_readings, axis=0))
    anomaly = segment_readings - center
    return center + jnp.dot(transform.T, anomaly, precision=highest_precision)

def assimilate(replica_dynamics_vector, cell_index, values, weight, listed, counts):
    owners = jnp.arange(NTILES, dtype=jnp.int32)[:, None] // PATCHES_PER_UNIT
    global_cells = (owners * CELLS_DEV + cell_index).astype(jnp.int32)
    picked = replica_dynamics_vector[:, global_cells]
    center = lax.optimization_barrier(jnp.mean(picked, axis=0))
    root_weight = jnp.sqrt(weight)
    spread = jnp.transpose((picked - center) * root_weight, (1, 0, 2))
    innovation = (values - center) * root_weight

    def one_block(block_index):
        segment_readings = lax.dynamic_slice_in_dim(replica_dynamics_vector, block_index * BLOCK, BLOCK, 1)
        chosen = listed[block_index]
        living = (jnp.arange(L_MAX, dtype=jnp.int32) < counts[block_index]).astype(jnp.float32)
        spreads = spread[chosen] * living[:, None, None]
        innovs = innovation[chosen] * living[:, None]
        return analyse_block(segment_readings, spreads, innovs)
    blocks = lax.map(one_block, jnp.arange(NBLK, dtype=jnp.int32))
    return jnp.transpose(blocks, (1, 0, 2)).reshape(ENSEMBLE_SIZE, GRID_CELLS)

def reference(initial_ensemble, driving_term, observation_cells, observation_values, observation_weight, block_tile_list, block_tile_count):
    replica_dynamics_vector = initial_ensemble
    for cycle_index in range(CYCLES):
        replica_dynamics_vector = background_prediction(replica_dynamics_vector, driving_term)
        for pass_index in range(PASSES):
            replica_dynamics_vector = assimilate(replica_dynamics_vector, observation_cells[cycle_index, pass_index], observation_values[cycle_index, pass_index], observation_weight[cycle_index, pass_index], block_tile_list[cycle_index, pass_index], block_tile_count[cycle_index, pass_index])
    return replica_dynamics_vector
```

```python
import functools
import math

import jax
import jax.numpy as jnp
from jax import lax
from jax.experimental import pallas as pl
from jax.experimental.pallas import tpu as pltpu
from jax.sharding import PartitionSpec as P

BLOCK = 512
NS_ITERS = 10
STEPS = 4
PASSES = 2
BEHIND = 2 * STEPS
AHEAD = STEPS

time_step = 0.05


def with_halo(cells, sides, width):
    for axis, dim in sides:
        count = lax.axis_size(axis)
        head = lax.slice_in_dim(cells, 0, width, axis=dim)
        tail = lax.slice_in_dim(cells, cells.shape[dim] - width, cells.shape[dim], axis=dim)
        cells = jnp.concatenate(
            [
                lax.ppermute(tail, axis, [(i, (i + 1) % count) for i in range(count)]),
                cells,
                lax.ppermute(head, axis, [((i + 1) % count, i) for i in range(count)]),
            ],
            axis=dim,
        )
    return cells


def forward_ring(count):
    return [(i, (i + 1) % count) for i in range(count)]


def backward_ring(count):
    return [((i + 1) % count, i) for i in range(count)]


def forecast(ensemble, driving_term):
    count = lax.axis_size("region")
    width = ensemble.shape[1]
    edge = jnp.concatenate(
        [ensemble, jnp.broadcast_to(driving_term[None], (8, width))], axis=0
    )
    behind = lax.ppermute(edge[:, width - BEHIND :], "region", forward_ring(count))
    ahead = lax.ppermute(edge[:, :AHEAD], "region", backward_ring(count))
    members = ensemble.shape[0]
    wide = jnp.concatenate([behind[:members], ensemble, ahead[:members]], axis=1)
    forcing = jnp.concatenate([behind[members], driving_term, ahead[members]])
    for _ in range(STEPS):
        inner = wide.shape[1] - 3
        wide = wide[:, 2 : inner + 2] + time_step * (
            (wide[:, 3:] - wide[:, :inner]) * wide[:, 1 : inner + 1]
            - wide[:, 2 : inner + 2]
            + forcing[2 : inner + 2]
        )
        forcing = forcing[2 : inner + 2]
    return wide


def split(value):
    high = value.astype(jnp.bfloat16)
    low = (value - high.astype(jnp.float32)).astype(jnp.bfloat16)
    return high, low


def dot3(left, right, contract=((1,), (0,))):
    def one(a, b):
        return lax.dot_general(
            a, b, (contract, ((), ())), preferred_element_type=jnp.float32
        )

    return one(left[0], right[0]) + (one(left[0], right[1]) + one(left[1], right[0]))


def roots(systems, identity):
    frobs = [jnp.sqrt(jnp.sum(s * s, keepdims=True)) for s in systems]
    firsts = [s / f for s, f in zip(systems, frobs)]

    def quartic(error):
        halves = split(error)
        square = dot3(halves, halves)
        rest = 0.375 * identity + 0.3125 * error + 0.0625 * square
        return 0.5 * error + dot3(split(square), split(rest))

    def close(inv, root):
        return identity - dot3(split(inv), split(root))

    invs, rts, errors = [], [], []
    for first in firsts:
        q = quartic(identity - first)
        invs.append(identity + q)
        rts.append(first + dot3(split(first), split(q)))
    errors = [close(i, r) for i, r in zip(invs, rts)]
    count = len(systems)

    def step(_, state):
        invs, rts, errors = state
        qs = [split(quartic(e)) for e in errors]
        invs = [i + dot3(split(i), q) for i, q in zip(invs, qs)]
        rts = [r + dot3(split(r), q) for r, q in zip(rts, qs)]
        return invs, rts, [close(i, r) for i, r in zip(invs, rts)]

    invs, rts, errors = lax.fori_loop(0, NS_ITERS // 2 - 2, step, (invs, rts, errors))
    qs = [split(quartic(e)) for e in errors]
    invs = [i + dot3(split(i), q) for i, q in zip(invs, qs)]
    return [i / jnp.sqrt(f) for i, f in zip(invs, frobs)]


def analysis_kernel(member_ref, tiles_ref, ens_ref, out_ref):
    blocks, tiles = member_ref.shape
    members = ens_ref.shape[0]
    rows = lax.broadcasted_iota(jnp.int32, (members, members), 0)
    columns = lax.broadcasted_iota(jnp.int32, (members, members), 1)
    identity = (rows == columns).astype(jnp.float32)
    grams = [(members - 1.0) * identity for _ in range(blocks)]
    pulls = [jnp.zeros((members, 1), jnp.float32) for _ in range(blocks)]
    for t in range(tiles):
        spread = tiles_ref[t, :members, :]
        innovation = tiles_ref[t, members : members + 1, :]
        halves = split(spread)
        gram = dot3(halves, halves, ((1,), (1,)))
        pull = jnp.sum(spread * innovation, axis=1, keepdims=True)
        for b in range(blocks):
            weight = member_ref[b, t]
            grams[b] = grams[b] + weight * gram
            pulls[b] = pulls[b] + weight * pull
    inv_roots = roots(grams, identity)
    for b in range(blocks):
        inv_root = inv_roots[b]
        inner = jnp.sum(inv_root * pulls[b], axis=0, keepdims=True)
        shift = jnp.sum(inv_root * inner, axis=1, keepdims=True)
        cells = ens_ref[:, b * BLOCK : (b + 1) * BLOCK]
        center = jnp.mean(cells, axis=0, keepdims=True)
        anomaly = cells - center
        base = center + jnp.sum(shift * anomaly, axis=0, keepdims=True)
        scaled = split(math.sqrt(members - 1) * inv_root)
        out_ref[:, b * BLOCK : (b + 1) * BLOCK] = base + dot3(scaled, split(anomaly))


def analyse(member_ship, nearby, ensemble):
    return pl.pallas_call(
        analysis_kernel,
        out_shape=jax.ShapeDtypeStruct(ensemble.shape, jnp.float32),
        in_specs=[
            pl.BlockSpec(memory_space=pltpu.SMEM),
            pl.BlockSpec(memory_space=pltpu.VMEM),
            pl.BlockSpec(memory_space=pltpu.VMEM),
        ],
        out_specs=pl.BlockSpec(memory_space=pltpu.VMEM),
    )(member_ship, nearby, ensemble)


def tile_pack(ensemble, cell_index, values, weight):
    picked = ensemble[:, cell_index]
    center = jnp.mean(picked, axis=0)
    root_weight = jnp.sqrt(weight)
    spread = (picked - center) * root_weight
    innovation = (values - center) * root_weight
    return jnp.concatenate([jnp.transpose(spread, (1, 0, 2)), innovation[:, None, :]], axis=1)


def memberships(listed, counts, device, devices, tiles_here):
    slot_ids = (listed - (device - 1) * tiles_here) % (devices * tiles_here)
    living = lax.broadcasted_iota(jnp.int32, listed.shape, 2) < counts[:, :, None]
    candidates = lax.broadcasted_iota(jnp.int32, (1, 1, 1, 3 * tiles_here), 3)
    chosen = living[..., None] & (slot_ids[..., None] == candidates)
    return jnp.sum(chosen.astype(jnp.float32), axis=2)


def local(
    initial_ensemble,
    driving_term,
    observation_cells,
    observation_values,
    observation_weight,
    block_tile_list,
    block_tile_count,
):
    device = lax.axis_index("region") * lax.axis_size("member") + lax.axis_index("member")
    devices = lax.axis_size("region") * lax.axis_size("member")
    tiles_here = observation_cells.shape[2]
    member_ship = memberships(block_tile_list[0], block_tile_count[0], device, devices, tiles_here)
    replica = forecast(initial_ensemble, driving_term)
    ensemble = lax.all_to_all(replica, "member", split_axis=1, concat_axis=0, tiled=True)
    for p in range(PASSES):
        packed = tile_pack(
            ensemble, observation_cells[0, p], observation_values[0, p], observation_weight[0, p]
        )
        nearby = with_halo(packed, ((("region", "member"), 0),), tiles_here)
        ensemble = analyse(member_ship[p], nearby, ensemble)
    return lax.all_to_all(ensemble, "member", split_axis=0, concat_axis=1, tiled=True)


def solution(mesh):
    in_specs = (
        P("member", "region"),
        P("region"),
        P(None, None, ("region", "member"), None),
        P(None, None, ("region", "member"), None),
        P(None, None, ("region", "member"), None),
        P(None, None, ("region", "member"), None),
        P(None, None, ("region", "member")),
    )
    out_specs = P("member", "region")
    return jax.shard_map(local, mesh=mesh, in_specs=in_specs, out_specs=out_specs, check_vma=False)
```

```python
import functools
import math

import jax
import jax.numpy as jnp
from jax import lax
from jax.experimental import pallas as pl
from jax.experimental.pallas import tpu as pltpu
from jax.sharding import PartitionSpec as P

BLOCK = 512
NS_ITERS = 10
STEPS = 4
PASSES = 2
LANES = 128
MESH = pl.DeviceIdType.MESH

time_step = 0.05


def split(value):
    high = value.astype(jnp.bfloat16)
    low = (value - high.astype(jnp.float32)).astype(jnp.bfloat16)
    return high, low


def dot3(left, right, contract=((1,), (0,))):
    wide = jnp.concatenate([left[0], left[0], left[1]], axis=contract[0][0])
    deep = jnp.concatenate([right[0], right[1], right[0]], axis=contract[1][0])
    return lax.dot_general(wide, deep, (contract, ((), ())), preferred_element_type=jnp.float32)


def roots(systems, identity):
    frobs = [jnp.sqrt(jnp.sum(s * s, keepdims=True)) for s in systems]
    firsts = [s / f for s, f in zip(systems, frobs)]

    def quartic(error):
        halves = split(error)
        square = dot3(halves, halves)
        rest = 0.375 * identity + 0.3125 * error + 0.0625 * square
        return 0.5 * error + dot3(split(square), split(rest))

    def close(inv, root):
        return identity - dot3(split(inv), split(root))

    invs, rts, errors = [], [], []
    for first in firsts:
        q = quartic(identity - first)
        invs.append(identity + q)
        rts.append(first + dot3(split(first), split(q)))
    errors = [close(i, r) for i, r in zip(invs, rts)]
    count = len(systems)

    def step(_, state):
        invs, rts, errors = state
        qs = [split(quartic(e)) for e in errors]
        invs = [i + dot3(split(i), q) for i, q in zip(invs, qs)]
        rts = [r + dot3(split(r), q) for r, q in zip(rts, qs)]
        return invs, rts, [close(i, r) for i, r in zip(invs, rts)]

    invs, rts, errors = lax.fori_loop(0, NS_ITERS // 2 - 2, step, (invs, rts, errors))
    qs = [split(quartic(e)) for e in errors]
    invs = [i + dot3(split(i), q) for i, q in zip(invs, qs)]
    return [i / jnp.sqrt(f) for i, f in zip(invs, frobs)]


def memberships(listed, counts, device, devices, tiles_here):
    slot_ids = (listed - (device - 1) * tiles_here) % (devices * tiles_here)
    living = lax.broadcasted_iota(jnp.int32, listed.shape, 2) < counts[:, :, None]
    candidates = lax.broadcasted_iota(jnp.int32, (1, 1, 1, 3 * tiles_here), 3)
    chosen = living[..., None] & (slot_ids[..., None] == candidates)
    return jnp.sum(chosen.astype(jnp.float32), axis=2)


def snake_member(position, count):
    half = count // 2
    late = position // half
    return 2 * position * (1 - late) + (2 * (count - 1 - position) + 1) * late


def snake_position(member, count):
    odd = member % 2
    return (member // 2) * (1 - odd) + (count - 1 - member // 2) * odd


def forecast_window(wide, forcing):
    width = wide.shape[1]
    for _ in range(STEPS):
        ahead_one = pltpu.roll(wide, width - 1, 1)
        behind = pltpu.roll(wide, 1, 1)
        further = pltpu.roll(wide, 2, 1)
        wide = wide + time_step * ((ahead_one - further) * behind - wide + forcing)
    return wide[:, LANES : width - LANES]


def kernel(
    count,
    regions,
    x_ref,
    drive_ref,
    obs_ref,
    out_ref,
    fc_ref,
    ens_ref,
    upd_ref,
    left_ref,
    right_ref,
    dleft_ref,
    dright_ref,
    own_obs,
    tiles_ref,
    halo_send,
    halo_recv,
    obs_send,
    obs_recv,
    in_send,
    in_recv,
    tile_send,
    tile_recv,
    out_send,
    out_recv,
    local_sem,
):
    region = lax.axis_index("region")
    me = lax.axis_index("member")
    position = snake_position(me, count)
    rows, cells = x_ref.shape
    members = ens_ref.shape[0]
    window = ens_ref.shape[1]
    up = (region + 1) % regions
    down = (region + regions - 1) % regions
    nxt = (
        (region + (position + 1) // count) % regions,
        snake_member((position + 1) % count, count),
    )
    before = (position + count - 1) % count
    prv = (
        (region + regions - (count - position) // count) % regions,
        snake_member(before, count),
    )

    barrier = pltpu.get_barrier_semaphore()

    def greet(target):
        pl.semaphore_signal(barrier, inc=1, device_id=target, device_id_type=MESH)

    for k in range(1, count):
        greet((region, (me + k) % count))
    for target in ((up, me), (down, me), nxt, prv):
        greet(target)
    pl.semaphore_wait(barrier, count + 3)

    def remote(source, target, send, recv, device):
        return pltpu.make_async_remote_copy(
            src_ref=source,
            dst_ref=target,
            send_sem=send,
            recv_sem=recv,
            device_id=device,
            device_id_type=MESH,
        )

    last = slice(cells - LANES, cells)
    halos = [
        remote(x_ref.at[:, last], left_ref, halo_send.at[0], halo_recv.at[0], (up, me)),
        remote(x_ref.at[:, 0:LANES], right_ref, halo_send.at[1], halo_recv.at[1], (down, me)),
        remote(drive_ref.at[:, last], dleft_ref, halo_send.at[2], halo_recv.at[2], (up, me)),
        remote(drive_ref.at[:, 0:LANES], dright_ref, halo_send.at[3], halo_recv.at[3], (down, me)),
    ]
    for copy in halos:
        copy.start()

    obs_home = snake_member(me, count)
    obs_copy = remote(obs_ref, own_obs, obs_send, obs_recv, (region, obs_home))
    obs_local = pltpu.make_async_copy(obs_ref, own_obs, local_sem.at[0])

    @pl.when(obs_home != me)
    def _():
        obs_copy.start()

    @pl.when(obs_home == me)
    def _():
        obs_local.start()

    my_rows = pl.ds(pl.multiple_of(me * rows, 8), rows)

    def in_copy(w):
        return remote(
            fc_ref.at[:, pl.ds(pl.multiple_of(w * window, LANES), window)],
            ens_ref.at[my_rows, :],
            in_send.at[w],
            in_recv.at[me],
            (region, snake_member(w, count)),
        )

    def own_window():
        return pltpu.make_async_copy(
            fc_ref.at[:, pl.ds(pl.multiple_of(position * window, LANES), window)],
            ens_ref.at[my_rows, :],
            local_sem.at[1],
        )

    def ship(w):
        @pl.when(w != position)
        def _():
            in_copy(w).start()

        @pl.when(w == position)
        def _():
            own_window().start()

    quarter = max(count // 4, 1)
    outer = ((position + quarter) // (2 * quarter)) % 2
    first = quarter * (1 + 2 * outer) - 1

    def interior(k, carry):
        w = 1 + (first + k) % (count - 2)
        span = pl.ds(pl.multiple_of(w * window - LANES, LANES), window + 2 * LANES)
        fc_ref[:, pl.ds(pl.multiple_of(w * window, LANES), window)] = forecast_window(
            x_ref[:, span], drive_ref[:, span]
        )
        ship(w)
        return carry

    lax.fori_loop(0, count - 2, interior, 0)
    for copy in halos:
        copy.wait()
    head = window + LANES
    fc_ref[:, 0:window] = forecast_window(
        jnp.concatenate([left_ref[...], x_ref[:, 0:head]], axis=1),
        jnp.concatenate([dleft_ref[...], drive_ref[:, 0:head]], axis=1),
    )
    ship(0)
    fc_ref[:, cells - window : cells] = forecast_window(
        jnp.concatenate([x_ref[:, cells - head : cells], right_ref[...]], axis=1),
        jnp.concatenate([drive_ref[:, cells - head : cells], dright_ref[...]], axis=1),
    )
    ship(count - 1)

    @pl.when(obs_home != me)
    def _():
        obs_copy.wait()

    @pl.when(obs_home == me)
    def _():
        obs_local.wait()

    own_window().wait()

    for k in range(1, count):
        sender = (me + k) % count
        remote(
            fc_ref.at[:, 0:window],
            ens_ref.at[pl.ds(pl.multiple_of(sender * rows, 8), rows), :],
            in_send.at[0],
            in_recv.at[sender],
            (region, sender),
        ).wait_recv()

    def sent_in(k, carry):
        in_copy((position + k) % count).wait_send()
        return carry

    lax.fori_loop(1, count, sent_in, 0)

    eye_rows = lax.broadcasted_iota(jnp.int32, (members, members), 0)
    eye_columns = lax.broadcasted_iota(jnp.int32, (members, members), 1)
    identity = (eye_rows == eye_columns).astype(jnp.float32)
    tiles = tiles_ref.shape[3] // LANES
    blocks = window // BLOCK
    place = lax.broadcasted_iota(jnp.int32, (window, LANES), 0)

    def obs_row(kind, p, t):
        r = (kind * PASSES + p) * tiles + t
        return own_obs[r : r + 1, :]

    def exchange(p):
        state = ens_ref[...]
        high, rest = split_rest(state)
        middle, rest = split_rest(rest)
        low = rest.astype(jnp.bfloat16)
        chosen = jnp.concatenate(
            [
                (place == obs_row(0, p, t).astype(jnp.int32)).astype(jnp.bfloat16)
                for t in range(tiles)
            ],
            axis=1,
        )

        def pick(part):
            return jnp.dot(part, chosen, preferred_element_type=jnp.float32)

        picked = pick(high) + (pick(middle) + pick(low))
        center = jnp.mean(picked, axis=0, keepdims=True)
        values = jnp.concatenate([obs_row(1, p, t) for t in range(tiles)], axis=1)
        weights = jnp.concatenate([obs_row(2, p, t) for t in range(tiles)], axis=1)
        root_weight = jnp.sqrt(weights)
        tiles_ref[p, 1, 0:members, :] = (picked - center) * root_weight
        tiles_ref[p, 1, members : members + 8, :] = jnp.broadcast_to(
            (values - center) * root_weight, (8, values.shape[1])
        )
        copies = [
            remote(
                tiles_ref.at[p, 1], tiles_ref.at[p, 0], tile_send.at[p, 0], tile_recv.at[p, 0], nxt
            ),
            remote(
                tiles_ref.at[p, 1], tiles_ref.at[p, 2], tile_send.at[p, 1], tile_recv.at[p, 1], prv
            ),
        ]
        for copy in copies:
            copy.start()
        return copies

    def gather_systems(p, copies):
        grams = [(members - 1.0) * identity for _ in range(blocks)]
        pulls = [jnp.zeros((members, 1), jnp.float32) for _ in range(blocks)]
        for owner in (1, 0, 2):
            if owner == 0:
                for copy in copies:
                    copy.wait()
            for t in range(tiles):
                lanes = slice(t * LANES, (t + 1) * LANES)
                spread = tiles_ref[p, owner, 0:members, lanes]
                innovation = tiles_ref[p, owner, members : members + 1, lanes]
                halves = split(spread)
                gram = dot3(halves, halves, ((1,), (1,)))
                pull = jnp.sum(spread * innovation, axis=1, keepdims=True)
                slot = owner * tiles + t
                for b in range(blocks):
                    weight = obs_row(3, p, b)[:, slot : slot + 1]
                    grams[b] = grams[b] + weight * gram
                    pulls[b] = pulls[b] + weight * pull
        return grams, pulls

    def apply(inv_root, pull, b):
        inner = jnp.sum(inv_root * pull, axis=0, keepdims=True)
        shift = jnp.sum(inv_root * inner, axis=1, keepdims=True)
        state = ens_ref[:, b * BLOCK : (b + 1) * BLOCK]
        center = jnp.mean(state, axis=0, keepdims=True)
        anomaly = state - center
        base = center + jnp.sum(shift * anomaly, axis=0, keepdims=True)
        scaled = split(math.sqrt(members - 1) * inv_root)
        return base + dot3(scaled, split(anomaly))

    for p in range(PASSES - 1):
        grams, pulls = gather_systems(p, exchange(p))
        inv_roots = roots(grams, identity)
        for b in range(blocks):
            ens_ref[:, b * BLOCK : (b + 1) * BLOCK] = apply(inv_roots[b], pulls[b], b)

    def out_copy(b, k):
        target = (me + k) % count
        return remote(
            upd_ref.at[
                pl.ds(pl.multiple_of(target * rows, 8), rows), b * BLOCK : (b + 1) * BLOCK
            ],
            out_ref.at[:, pl.ds(pl.multiple_of(position * window + b * BLOCK, LANES), BLOCK)],
            out_send.at[b, k],
            out_recv.at[b, me],
            (region, target),
        )

    def out_own(b):
        return pltpu.make_async_copy(
            upd_ref.at[my_rows, b * BLOCK : (b + 1) * BLOCK],
            out_ref.at[:, pl.ds(pl.multiple_of(position * window + b * BLOCK, LANES), BLOCK)],
            local_sem.at[2 + b],
        )

    p = PASSES - 1
    grams, pulls = gather_systems(p, exchange(p))
    order = [(count // 2 + k) % count for k in range(count)]
    for b in range(blocks):
        (inv_root,) = roots([grams[b]], identity)
        upd_ref[:, b * BLOCK : (b + 1) * BLOCK] = apply(inv_root, pulls[b], b)
        for k in order:
            if k:
                out_copy(b, k).start()
        out_own(b).start()
    for b in range(blocks):
        for k in range(1, count):
            sender = (me + k) % count
            remote(
                upd_ref.at[0:rows, b * BLOCK : (b + 1) * BLOCK],
                out_ref.at[
                    :,
                    pl.ds(
                        pl.multiple_of(
                            snake_position(sender, count) * window + b * BLOCK, LANES
                        ),
                        BLOCK,
                    ),
                ],
                out_send.at[b, 0],
                out_recv.at[b, sender],
                (region, sender),
            ).wait_recv()
        for k in range(1, count):
            out_copy(b, k).wait_send()
        out_own(b).wait()


def split_rest(value):
    high = value.astype(jnp.bfloat16)
    return high, value - high.astype(jnp.float32)


def local(
    initial_ensemble,
    driving_term,
    observation_cells,
    observation_values,
    observation_weight,
    block_tile_list,
    block_tile_count,
):
    count = lax.axis_size("member")
    regions = lax.axis_size("region")
    device = lax.axis_index("region") * count + lax.axis_index("member")
    tiles_here = observation_cells.shape[2]
    rows, cells = initial_ensemble.shape
    members = rows * count
    window = cells // count
    blocks = window // BLOCK
    member_ship = memberships(
        block_tile_list[0], block_tile_count[0], device, count * regions, tiles_here
    )
    slots = member_ship.shape[2]
    obs = jnp.concatenate(
        [
            observation_cells[0].astype(jnp.float32).reshape(-1, LANES),
            observation_values[0].reshape(-1, LANES),
            observation_weight[0].reshape(-1, LANES),
            jnp.pad(member_ship.reshape(-1, slots), ((0, 0), (0, LANES - slots))),
        ]
    )
    vmem = pl.BlockSpec(memory_space=pltpu.VMEM)
    f32 = jnp.float32
    dma = pltpu.SemaphoreType.DMA
    return pl.pallas_call(
        functools.partial(kernel, count, regions),
        out_shape=jax.ShapeDtypeStruct((rows, cells), f32),
        in_specs=[vmem, vmem, vmem],
        out_specs=vmem,
        scratch_shapes=[
            pltpu.VMEM((rows, cells), f32),
            pltpu.VMEM((members, window), f32),
            pltpu.VMEM((members, window), f32),
            pltpu.VMEM((rows, LANES), f32),
            pltpu.VMEM((rows, LANES), f32),
            pltpu.VMEM((1, LANES), f32),
            pltpu.VMEM((1, LANES), f32),
            pltpu.VMEM(obs.shape, f32),
            pltpu.VMEM((PASSES, 3, members + 8, tiles_here * LANES), f32),
            dma((4,)),
            dma((4,)),
            dma,
            dma,
            dma((count,)),
            dma((count,)),
            dma((PASSES, 2)),
            dma((PASSES, 2)),
            dma((blocks, count)),
            dma((blocks, count)),
            dma((2 + blocks,)),
        ],
        compiler_params=pltpu.CompilerParams(
            collective_id=0, has_side_effects=True, vmem_limit_bytes=48 * 1024 * 1024
        ),
    )(initial_ensemble, driving_term[None], obs)


def solution(mesh):
    in_specs = (
        P("member", "region"),
        P("region"),
        P(None, None, ("region", "member"), None),
        P(None, None, ("region", "member"), None),
        P(None, None, ("region", "member"), None),
        P(None, None, ("region", "member"), None),
        P(None, None, ("region", "member")),
    )
    out_specs = P("member", "region")
    return jax.shard_map(local, mesh=mesh, in_specs=in_specs, out_specs=out_specs, check_vma=False)
```

```python
import functools
import math

import jax
import jax.numpy as jnp
from jax import lax
from jax.experimental import pallas as pl
from jax.experimental.pallas import tpu as pltpu
from jax.sharding import PartitionSpec as P

BLOCK = 512
NS_ITERS = 10
STEPS = 4
PASSES = 2
LANES = 128
MESH = pl.DeviceIdType.MESH

time_step = 0.05


def split(value):
    high = value.astype(jnp.bfloat16)
    low = (value - high.astype(jnp.float32)).astype(jnp.bfloat16)
    return high, low


def dot3(left, right, contract=((1,), (0,))):
    wide = jnp.concatenate([left[0], left[0], left[1]], axis=contract[0][0])
    deep = jnp.concatenate([right[0], right[1], right[0]], axis=contract[1][0])
    return lax.dot_general(wide, deep, (contract, ((), ())), preferred_element_type=jnp.float32)


def roots(systems, identity):
    frobs = [jnp.sqrt(jnp.sum(s * s, keepdims=True)) for s in systems]
    firsts = [s / f for s, f in zip(systems, frobs)]

    def quartic(error):
        halves = split(error)
        square = dot3(halves, halves)
        rest = 0.375 * identity + 0.3125 * error + 0.0625 * square
        return 0.5 * error + dot3(split(square), split(rest))

    def close(inv, root):
        return identity - dot3(split(inv), split(root))

    invs, rts, errors = [], [], []
    for first in firsts:
        q = quartic(identity - first)
        invs.append(identity + q)
        rts.append(first + dot3(split(first), split(q)))
    errors = [close(i, r) for i, r in zip(invs, rts)]
    count = len(systems)

    def step(_, state):
        invs, rts, errors = state
        qs = [split(quartic(e)) for e in errors]
        invs = [i + dot3(split(i), q) for i, q in zip(invs, qs)]
        rts = [r + dot3(split(r), q) for r, q in zip(rts, qs)]
        return invs, rts, [close(i, r) for i, r in zip(invs, rts)]

    invs, rts, errors = lax.fori_loop(0, NS_ITERS // 2 - 2, step, (invs, rts, errors))
    qs = [split(quartic(e)) for e in errors]
    invs = [i + dot3(split(i), q) for i, q in zip(invs, qs)]
    return [i / jnp.sqrt(f) for i, f in zip(invs, frobs)]


def snake_member(position, count):
    half = count // 2
    late = position // half
    return 2 * position * (1 - late) + (2 * (count - 1 - position) + 1) * late


def snake_position(member, count):
    odd = member % 2
    return (member // 2) * (1 - odd) + (count - 1 - member // 2) * odd


def forecast_window(wide, forcing):
    width = wide.shape[1]
    for _ in range(STEPS):
        ahead_one = pltpu.roll(wide, width - 1, 1)
        behind = pltpu.roll(wide, 1, 1)
        further = pltpu.roll(wide, 2, 1)
        wide = wide + time_step * ((ahead_one - further) * behind - wide + forcing)
    return wide[:, LANES : width - LANES]


def kernel(
    count,
    regions,
    x_ref,
    drive_ref,
    cells_ref,
    values_ref,
    weights_ref,
    list_ref,
    counts_ref,
    out_ref,
    held_ref,
    fc_ref,
    ens_ref,
    upd_ref,
    dheld_ref,
    own_cells,
    own_values,
    own_weights,
    own_list,
    own_counts,
    tiles_ref,
    load_sem,
    halo_send,
    halo_recv,
    obs_send,
    obs_recv,
    in_send,
    in_recv,
    tile_send,
    tile_recv,
    out_send,
    out_recv,
    local_sem,
):
    region = lax.axis_index("region")
    me = lax.axis_index("member")
    rows = fc_ref.shape[0]
    cells = fc_ref.shape[1]
    members = ens_ref.shape[0]
    window = ens_ref.shape[1]
    up = (region + 1) % regions
    down = (region + regions - 1) % regions
    base = region - region % 2
    across = 2 * count
    mine = 2 * snake_position(me, count) + region % 2
    source_region = base + mine // count
    position = mine % count
    offset = (region % 2) * count

    def host(place):
        return (base + place % 2, snake_member(place // 2, count))

    nxt_place = (mine + 1) % across
    nxt = (
        (base + 2 * ((mine + 1) // across) + nxt_place % 2) % regions,
        snake_member(nxt_place // 2, count),
    )
    prv_place = (mine + across - 1) % across
    prv = (
        (base + regions - 2 * ((across - mine) // across) + prv_place % 2) % regions,
        snake_member(prv_place // 2, count),
    )

    def load(w):
        span = pl.ds(pl.multiple_of(w * window, LANES), window)
        kept = pl.ds(pl.multiple_of(w * window + LANES, LANES), window)
        return pltpu.make_async_copy(x_ref.at[:, span], held_ref.at[:, kept], load_sem.at[w])

    def load_all(w, carry):
        load(w).start()
        return carry

    drive_load = pltpu.make_async_copy(
        drive_ref, dheld_ref.at[:, LANES : LANES + cells], local_sem.at[0]
    )
    drive_load.start()
    lax.fori_loop(0, count, load_all, 0)

    barrier = pltpu.get_barrier_semaphore()

    def greet(target):
        pl.semaphore_signal(barrier, inc=1, device_id=target, device_id_type=MESH)

    for k in range(count):
        greet((base + 1 - region % 2, (me + k) % count))
        if k:
            greet((region, (me + k) % count))
    for target in ((up, me), (down, me), nxt, prv):
        greet(target)
    pl.semaphore_wait(barrier, across + 3)

    def remote(source, target, send, recv, device):
        return pltpu.make_async_remote_copy(
            src_ref=source,
            dst_ref=target,
            send_sem=send,
            recv_sem=recv,
            device_id=device,
            device_id_type=MESH,
        )

    last = slice(cells - LANES, cells)
    end = LANES + cells
    halos = [
        remote(
            x_ref.at[:, last], held_ref.at[:, 0:LANES], halo_send.at[0], halo_recv.at[0], (up, me)
        ),
        remote(
            x_ref.at[:, 0:LANES],
            held_ref.at[:, end : end + LANES],
            halo_send.at[1],
            halo_recv.at[1],
            (down, me),
        ),
        remote(
            drive_ref.at[:, last],
            dheld_ref.at[:, 0:LANES],
            halo_send.at[2],
            halo_recv.at[2],
            (up, me),
        ),
        remote(
            drive_ref.at[:, 0:LANES],
            dheld_ref.at[:, end : end + LANES],
            halo_send.at[3],
            halo_recv.at[3],
            (down, me),
        ),
    ]
    for copy in halos:
        copy.start()

    obs_stays = (offset + me) == mine
    obs_pairs = (
        (cells_ref, own_cells),
        (values_ref, own_values),
        (weights_ref, own_weights),
        (list_ref, own_list),
        (counts_ref, own_counts),
    )
    obs_copies = [
        remote(source, target, obs_send.at[i], obs_recv.at[i], host(offset + me))
        for i, (source, target) in enumerate(obs_pairs)
    ]
    obs_locals = [
        pltpu.make_async_copy(source, target, obs_send.at[i])
        for i, (source, target) in enumerate(obs_pairs)
    ]

    @pl.when(jnp.logical_not(obs_stays))
    def _():
        for copy in obs_copies:
            copy.start()

    @pl.when(obs_stays)
    def _():
        for copy in obs_locals:
            copy.start()

    my_rows = pl.ds(pl.multiple_of(me * rows, 8), rows)

    def in_copy(w):
        return remote(
            fc_ref.at[:, pl.ds(pl.multiple_of(w * window, LANES), window)],
            ens_ref.at[my_rows, :],
            in_send.at[w],
            in_recv.at[me],
            host(offset + w),
        )

    def own_window():
        return pltpu.make_async_copy(
            fc_ref.at[:, pl.ds(pl.multiple_of(position * window, LANES), window)],
            ens_ref.at[my_rows, :],
            local_sem.at[1],
        )

    def ship(w):
        @pl.when(offset + w != mine)
        def _():
            in_copy(w).start()

        @pl.when(offset + w == mine)
        def _():
            own_window().start()

    def forecast_at(w):
        wide = pl.ds(pl.multiple_of(w * window, LANES), window + 2 * LANES)
        fc_ref[:, pl.ds(pl.multiple_of(w * window, LANES), window)] = forecast_window(
            held_ref[:, wide], dheld_ref[:, wide]
        )
        ship(w)

    def loaded(w, carry):
        load(w).wait()
        return carry

    def interior(k, carry):
        forecast_at(1 + (first + k) % (count - 2))
        return carry

    quarter = max(count // 4, 1)
    near = snake_position(me, count)
    outer = ((near + quarter) // (2 * quarter)) % 2
    first = (count // 2 - 1) * ((outer + region + 1) % 2)
    drive_load.wait()
    lax.fori_loop(0, count, loaded, 0)
    lax.fori_loop(0, count - 2, interior, 0)
    for copy in halos:
        copy.wait()
    forecast_at(0)
    forecast_at(count - 1)

    @pl.when(jnp.logical_not(obs_stays))
    def _():
        for copy in obs_copies:
            copy.wait()

    @pl.when(obs_stays)
    def _():
        for copy in obs_locals:
            copy.wait()

    def arrived(sender, carry):
        @pl.when((sender != me) | (source_region != region))
        def _():
            remote(
                fc_ref.at[:, 0:window],
                ens_ref.at[pl.ds(pl.multiple_of(sender * rows, 8), rows), :],
                in_send.at[0],
                in_recv.at[sender],
                (source_region, sender),
            ).wait_recv()

        return carry

    def sent_in(w, carry):
        @pl.when(offset + w != mine)
        def _():
            in_copy(w).wait_send()

        @pl.when(offset + w == mine)
        def _():
            own_window().wait()

        return carry

    lax.fori_loop(0, count, sent_in, 0)
    lax.fori_loop(0, count, arrived, 0)

    eye_rows = lax.broadcasted_iota(jnp.int32, (members, members), 0)
    eye_columns = lax.broadcasted_iota(jnp.int32, (members, members), 1)
    identity = (eye_rows == eye_columns).astype(jnp.float32)
    tiles = tiles_ref.shape[3] // LANES
    blocks = window // BLOCK
    place = lax.broadcasted_iota(jnp.int32, (window, LANES), 0)

    flat = base * count + mine
    devices = regions * count
    near_tiles = [
        ((flat + devices - 1 + slot // tiles) % devices) * tiles + slot % tiles
        for slot in range(3 * tiles)
    ]

    def share(p, b, slot):
        listed = own_list[0, p, b : b + 1, :]
        live = lax.broadcasted_iota(jnp.int32, listed.shape, 1) < own_counts[0, p : p + 1, b : b + 1]
        hits = live & (listed == near_tiles[slot])
        return jnp.sum(hits.astype(jnp.float32), axis=1, keepdims=True)

    def exchange(p):
        state = ens_ref[...]
        high, rest = split_rest(state)
        middle, rest = split_rest(rest)
        low = rest.astype(jnp.bfloat16)
        chosen = jnp.concatenate(
            [
                (place == own_cells[0, p, t : t + 1, :]).astype(jnp.bfloat16)
                for t in range(tiles)
            ],
            axis=1,
        )

        def pick(part):
            return jnp.dot(part, chosen, preferred_element_type=jnp.float32)

        picked = pick(high) + (pick(middle) + pick(low))
        center = jnp.mean(picked, axis=0, keepdims=True)
        values = jnp.concatenate([own_values[0, p, t : t + 1, :] for t in range(tiles)], axis=1)
        weights = jnp.concatenate([own_weights[0, p, t : t + 1, :] for t in range(tiles)], axis=1)
        root_weight = jnp.sqrt(weights)
        tiles_ref[p, 1, 0:members, :] = (picked - center) * root_weight
        tiles_ref[p, 1, members : members + 8, :] = jnp.broadcast_to(
            (values - center) * root_weight, (8, values.shape[1])
        )
        copies = [
            remote(
                tiles_ref.at[p, 1], tiles_ref.at[p, 0], tile_send.at[p, 0], tile_recv.at[p, 0], nxt
            ),
            remote(
                tiles_ref.at[p, 1], tiles_ref.at[p, 2], tile_send.at[p, 1], tile_recv.at[p, 1], prv
            ),
        ]
        for copy in copies:
            copy.start()
        return copies

    def gather_systems(p, copies):
        grams = [(members - 1.0) * identity for _ in range(blocks)]
        pulls = [jnp.zeros((members, 1), jnp.float32) for _ in range(blocks)]
        for owner in (1, 0, 2):
            if owner == 0:
                for copy in copies:
                    copy.wait()
            for t in range(tiles):
                lanes = slice(t * LANES, (t + 1) * LANES)
                spread = tiles_ref[p, owner, 0:members, lanes]
                innovation = tiles_ref[p, owner, members : members + 1, lanes]
                halves = split(spread)
                gram = dot3(halves, halves, ((1,), (1,)))
                pull = jnp.sum(spread * innovation, axis=1, keepdims=True)
                slot = owner * tiles + t
                for b in range(blocks):
                    weight = share(p, b, slot)
                    grams[b] = grams[b] + weight * gram
                    pulls[b] = pulls[b] + weight * pull
        return grams, pulls

    def apply(inv_root, pull, b):
        inner = jnp.sum(inv_root * pull, axis=0, keepdims=True)
        shift = jnp.sum(inv_root * inner, axis=1, keepdims=True)
        state = ens_ref[:, b * BLOCK : (b + 1) * BLOCK]
        center = jnp.mean(state, axis=0, keepdims=True)
        anomaly = state - center
        base = center + jnp.sum(shift * anomaly, axis=0, keepdims=True)
        scaled = split(math.sqrt(members - 1) * inv_root)
        return base + dot3(scaled, split(anomaly))

    for p in range(PASSES - 1):
        grams, pulls = gather_systems(p, exchange(p))
        inv_roots = roots(grams, identity)
        for b in range(blocks):
            ens_ref[:, b * BLOCK : (b + 1) * BLOCK] = apply(inv_roots[b], pulls[b], b)

    here = pl.multiple_of(position * window, LANES)

    def out_copy(b, target):
        return remote(
            upd_ref.at[
                pl.ds(pl.multiple_of(target * rows, 8), rows), b * BLOCK : (b + 1) * BLOCK
            ],
            out_ref.at[:, pl.ds(here + b * BLOCK, BLOCK)],
            out_send.at[b, target],
            out_recv.at[b, position],
            (source_region, target),
        )

    def out_own(b):
        return pltpu.make_async_copy(
            upd_ref.at[my_rows, b * BLOCK : (b + 1) * BLOCK],
            out_ref.at[:, pl.ds(here + b * BLOCK, BLOCK)],
            local_sem.at[2 + b],
        )

    def each_target(b, remote_step, local_step):
        def go(k, carry):
            target = (me + count // 2 + k) % count
            stays = (target == me) & (source_region == region)

            @pl.when(jnp.logical_not(stays))
            def _():
                remote_step(out_copy(b, target))

            @pl.when(stays)
            def _():
                local_step(out_own(b))

            return carry

        lax.fori_loop(0, count, go, 0)

    p = PASSES - 1
    grams, pulls = gather_systems(p, exchange(p))
    for b in range(blocks):
        (inv_root,) = roots([grams[b]], identity)
        upd_ref[:, b * BLOCK : (b + 1) * BLOCK] = apply(inv_root, pulls[b], b)
        each_target(b, lambda copy: copy.start(), lambda copy: copy.start())

    for b in range(blocks):
        each_target(b, lambda copy: copy.wait_send(), lambda copy: copy.wait())

        def landed(w, carry):
            @pl.when(offset + w != mine)
            def _():
                remote(
                    upd_ref.at[0:rows, b * BLOCK : (b + 1) * BLOCK],
                    out_ref.at[
                        :, pl.ds(pl.multiple_of(w * window + b * BLOCK, LANES), BLOCK)
                    ],
                    out_send.at[b, 0],
                    out_recv.at[b, w],
                    host(offset + w),
                ).wait_recv()

            return carry

        lax.fori_loop(0, count, landed, 0)


def split_rest(value):
    high = value.astype(jnp.bfloat16)
    return high, value - high.astype(jnp.float32)


def local(
    initial_ensemble,
    driving_term,
    observation_cells,
    observation_values,
    observation_weight,
    block_tile_list,
    block_tile_count,
):
    count = lax.axis_size("member")
    regions = lax.axis_size("region")
    tiles_here = observation_cells.shape[2]
    rows, cells = initial_ensemble.shape
    members = rows * count
    window = cells // count
    blocks = window // BLOCK
    kept = pl.BlockSpec(memory_space=pl.ANY)
    wide = cells + 2 * LANES
    f32 = jnp.float32
    dma = pltpu.SemaphoreType.DMA
    return pl.pallas_call(
        functools.partial(kernel, count, regions),
        out_shape=jax.ShapeDtypeStruct((rows, cells), f32),
        in_specs=[kept] * 7,
        out_specs=kept,
        scratch_shapes=[
            pltpu.VMEM((rows, wide), f32),
            pltpu.VMEM((rows, cells), f32),
            pltpu.VMEM((members, window), f32),
            pltpu.VMEM((members, window), f32),
            pltpu.VMEM((1, wide), f32),
            pltpu.VMEM(observation_cells.shape, jnp.int32),
            pltpu.VMEM(observation_values.shape, f32),
            pltpu.VMEM(observation_weight.shape, f32),
            pltpu.VMEM(block_tile_list.shape, jnp.int32),
            pltpu.VMEM(block_tile_count.shape, jnp.int32),
            pltpu.VMEM((PASSES, 3, members + 8, tiles_here * LANES), f32),
            dma((count,)),
            dma((4,)),
            dma((4,)),
            dma((5,)),
            dma((5,)),
            dma((count,)),
            dma((count,)),
            dma((PASSES, 2)),
            dma((PASSES, 2)),
            dma((blocks, count)),
            dma((blocks, count)),
            dma((2 + blocks,)),
        ],
        compiler_params=pltpu.CompilerParams(
            collective_id=0, has_side_effects=True, vmem_limit_bytes=67_043_328
        ),
    )(
        initial_ensemble,
        driving_term[None],
        observation_cells,
        observation_values,
        observation_weight,
        block_tile_list,
        block_tile_count,
    )


def solution(mesh):
    in_specs = (
        P("member", "region"),
        P("region"),
        P(None, None, ("region", "member"), None),
        P(None, None, ("region", "member"), None),
        P(None, None, ("region", "member"), None),
        P(None, None, ("region", "member"), None),
        P(None, None, ("region", "member")),
    )
    out_specs = P("member", "region")
    return jax.shard_map(local, mesh=mesh, in_specs=in_specs, out_specs=out_specs, check_vma=False)
```

```python
import functools
import math

import jax
import jax.numpy as jnp
from jax import lax
from jax.experimental import pallas as pl
from jax.experimental.pallas import tpu as pltpu
from jax.sharding import PartitionSpec as P

BLOCK = 512
NS_ITERS = 10
STEPS = 4
PASSES = 2
LANES = 128
MESH = pl.DeviceIdType.MESH

time_step = 0.05


def split(value):
    high = value.astype(jnp.bfloat16)
    low = (value - high.astype(jnp.float32)).astype(jnp.bfloat16)
    return high, low


def dot3(left, right, contract=((1,), (0,))):
    wide = jnp.concatenate([left[0], left[0], left[1]], axis=contract[0][0])
    deep = jnp.concatenate([right[0], right[1], right[0]], axis=contract[1][0])
    return lax.dot_general(wide, deep, (contract, ((), ())), preferred_element_type=jnp.float32)


def roots(systems, identity):
    frobs = [jnp.sqrt(jnp.sum(s * s, keepdims=True)) for s in systems]
    firsts = [s / f for s, f in zip(systems, frobs)]

    def quartic(error):
        halves = split(error)
        square = dot3(halves, halves)
        rest = 0.375 * identity + 0.3125 * error + 0.0625 * square
        return 0.5 * error + dot3(split(square), split(rest))

    def close(inv, root):
        return identity - dot3(split(inv), split(root))

    invs, rts, errors = [], [], []
    for first in firsts:
        q = quartic(identity - first)
        invs.append(identity + q)
        rts.append(first + dot3(split(first), split(q)))
    errors = [close(i, r) for i, r in zip(invs, rts)]
    count = len(systems)

    def step(_, state):
        invs, rts, errors = state
        qs = [split(quartic(e)) for e in errors]
        invs = [i + dot3(split(i), q) for i, q in zip(invs, qs)]
        rts = [r + dot3(split(r), q) for r, q in zip(rts, qs)]
        return invs, rts, [close(i, r) for i, r in zip(invs, rts)]

    invs, rts, errors = lax.fori_loop(
        0, NS_ITERS // 2 - 2, step, (invs, rts, errors), unroll=True
    )
    qs = [split(quartic(e)) for e in errors]
    invs = [i + dot3(split(i), q) for i, q in zip(invs, qs)]
    return [i / jnp.sqrt(f) for i, f in zip(invs, frobs)]


def snake_member(position, count):
    half = count // 2
    late = position // half
    return 2 * position * (1 - late) + (2 * (count - 1 - position) + 1) * late


def snake_position(member, count):
    odd = member % 2
    return (member // 2) * (1 - odd) + (count - 1 - member // 2) * odd


def forecast_window(wide, forcing):
    width = wide.shape[1]
    for _ in range(STEPS):
        ahead_one = pltpu.roll(wide, width - 1, 1)
        behind = pltpu.roll(wide, 1, 1)
        further = pltpu.roll(wide, 2, 1)
        wide = wide + time_step * ((ahead_one - further) * behind - wide + forcing)
    return wide[:, LANES : width - LANES]


def kernel(
    count,
    regions,
    x_ref,
    drive_ref,
    cells_ref,
    values_ref,
    weights_ref,
    list_ref,
    counts_ref,
    out_ref,
    held_ref,
    fc_ref,
    ens_ref,
    upd_ref,
    dheld_ref,
    own_cells,
    own_values,
    own_weights,
    own_list,
    own_counts,
    tiles_ref,
    chosen_ref,
    load_sem,
    halo_send,
    halo_recv,
    obs_send,
    obs_recv,
    in_send,
    in_recv,
    tile_send,
    tile_recv,
    out_send,
    out_recv,
    local_sem,
):
    region = lax.axis_index("region")
    me = lax.axis_index("member")
    rows = fc_ref.shape[0]
    cells = fc_ref.shape[1]
    members = ens_ref.shape[0]
    window = ens_ref.shape[1]
    up = (region + 1) % regions
    down = (region + regions - 1) % regions
    base = region - region % 2
    across = 2 * count
    mine = 2 * snake_position(me, count) + region % 2
    source_region = base + mine // count
    position = mine % count
    offset = (region % 2) * count

    def host(place):
        return (base + place % 2, snake_member(place // 2, count))

    nxt_place = (mine + 1) % across
    nxt = (
        (base + 2 * ((mine + 1) // across) + nxt_place % 2) % regions,
        snake_member(nxt_place // 2, count),
    )
    prv_place = (mine + across - 1) % across
    prv = (
        (base + regions - 2 * ((across - mine) // across) + prv_place % 2) % regions,
        snake_member(prv_place // 2, count),
    )

    def load(w):
        span = pl.ds(pl.multiple_of(w * window, LANES), window)
        kept = pl.ds(pl.multiple_of(w * window + LANES, LANES), window)
        return pltpu.make_async_copy(x_ref.at[:, span], held_ref.at[:, kept], load_sem.at[w])

    def load_all(w, carry):
        load(w).start()
        return carry

    drive_load = pltpu.make_async_copy(
        drive_ref, dheld_ref.at[:, LANES : LANES + cells], local_sem.at[0]
    )
    drive_load.start()
    lax.fori_loop(0, count, load_all, 0)

    barrier = pltpu.get_barrier_semaphore()

    def greet(target):
        pl.semaphore_signal(barrier, inc=1, device_id=target, device_id_type=MESH)

    for k in range(count):
        greet((base + 1 - region % 2, (me + k) % count))
        if k:
            greet((region, (me + k) % count))
    for target in ((up, me), (down, me), nxt, prv):
        greet(target)
    pl.semaphore_wait(barrier, across + 3)

    def remote(source, target, send, recv, device):
        return pltpu.make_async_remote_copy(
            src_ref=source,
            dst_ref=target,
            send_sem=send,
            recv_sem=recv,
            device_id=device,
            device_id_type=MESH,
        )

    last = slice(cells - LANES, cells)
    end = LANES + cells
    halos = [
        remote(
            x_ref.at[:, last], held_ref.at[:, 0:LANES], halo_send.at[0], halo_recv.at[0], (up, me)
        ),
        remote(
            x_ref.at[:, 0:LANES],
            held_ref.at[:, end : end + LANES],
            halo_send.at[1],
            halo_recv.at[1],
            (down, me),
        ),
        remote(
            drive_ref.at[:, last],
            dheld_ref.at[:, 0:LANES],
            halo_send.at[2],
            halo_recv.at[2],
            (up, me),
        ),
        remote(
            drive_ref.at[:, 0:LANES],
            dheld_ref.at[:, end : end + LANES],
            halo_send.at[3],
            halo_recv.at[3],
            (down, me),
        ),
    ]
    for copy in halos:
        copy.start()

    obs_stays = (offset + me) == mine
    obs_pairs = (
        (cells_ref, own_cells),
        (values_ref, own_values),
        (weights_ref, own_weights),
        (list_ref, own_list),
        (counts_ref, own_counts),
    )
    obs_copies = [
        remote(source, target, obs_send.at[i], obs_recv.at[i], host(offset + me))
        for i, (source, target) in enumerate(obs_pairs)
    ]
    obs_locals = [
        pltpu.make_async_copy(source, target, obs_send.at[i])
        for i, (source, target) in enumerate(obs_pairs)
    ]

    @pl.when(jnp.logical_not(obs_stays))
    def _():
        for copy in obs_copies:
            copy.start()

    @pl.when(obs_stays)
    def _():
        for copy in obs_locals:
            copy.start()

    my_rows = pl.ds(pl.multiple_of(me * rows, 8), rows)

    def in_copy(w):
        return remote(
            fc_ref.at[:, pl.ds(pl.multiple_of(w * window, LANES), window)],
            ens_ref.at[my_rows, :],
            in_send.at[w],
            in_recv.at[me],
            host(offset + w),
        )

    def own_window():
        return pltpu.make_async_copy(
            fc_ref.at[:, pl.ds(pl.multiple_of(position * window, LANES), window)],
            ens_ref.at[my_rows, :],
            local_sem.at[1],
        )

    def ship(w):
        @pl.when(offset + w != mine)
        def _():
            in_copy(w).start()

        @pl.when(offset + w == mine)
        def _():
            own_window().start()

    def forecast_at(w):
        wide = pl.ds(pl.multiple_of(w * window, LANES), window + 2 * LANES)
        fc_ref[:, pl.ds(pl.multiple_of(w * window, LANES), window)] = forecast_window(
            held_ref[:, wide], dheld_ref[:, wide]
        )
        ship(w)

    def loaded(w, carry):
        load(w).wait()
        return carry

    def interior(k, carry):
        forecast_at(1 + (first + k) % (count - 2))
        return carry

    quarter = max(count // 4, 1)
    near = snake_position(me, count)
    outer = ((near + quarter) // (2 * quarter)) % 2
    first = (count // 2 - 1) * ((outer + region + 1) % 2)
    drive_load.wait()
    lax.fori_loop(0, count, loaded, 0)
    lax.fori_loop(0, count - 2, interior, 0)
    for copy in halos:
        copy.wait()
    forecast_at(0)
    forecast_at(count - 1)

    @pl.when(jnp.logical_not(obs_stays))
    def _():
        for copy in obs_copies:
            copy.wait()

    @pl.when(obs_stays)
    def _():
        for copy in obs_locals:
            copy.wait()

    tiles = tiles_ref.shape[3] // LANES
    place = lax.broadcasted_iota(jnp.int32, (window, LANES), 0)
    for p in range(PASSES):
        for t in range(tiles):
            hit = place == own_cells[0, p, t : t + 1, :]
            chosen_ref[p, :, t * LANES : (t + 1) * LANES] = hit.astype(jnp.bfloat16)

    def pick(p, state):
        high, rest = split_rest(state)
        middle, rest = split_rest(rest)
        low = rest.astype(jnp.bfloat16)
        terms = jnp.concatenate([high, middle, low], axis=0)
        found = jnp.dot(terms, chosen_ref[p], preferred_element_type=jnp.float32)
        n = state.shape[0]
        return found[:n] + (found[n : 2 * n] + found[2 * n :])

    def arrived(k, carry):
        sender = (me + k) % count
        theirs = pl.ds(pl.multiple_of(sender * rows, 8), rows)
        local_rows = (sender == me) & (source_region == region)

        @pl.when(jnp.logical_not(local_rows))
        def _():
            remote(
                fc_ref.at[:, 0:window],
                ens_ref.at[theirs, :],
                in_send.at[0],
                in_recv.at[sender],
                (source_region, sender),
            ).wait_recv()

        @pl.when(local_rows)
        def _():
            own_window().wait()

        tiles_ref[0, 1, theirs, :] = pick(0, ens_ref[theirs, :])
        return carry

    def sent_in(w, carry):
        @pl.when(offset + w != mine)
        def _():
            in_copy(w).wait_send()

        return carry

    lax.fori_loop(0, count, arrived, 0)

    eye_rows = lax.broadcasted_iota(jnp.int32, (members, members), 0)
    eye_columns = lax.broadcasted_iota(jnp.int32, (members, members), 1)
    identity = (eye_rows == eye_columns).astype(jnp.float32)
    blocks = window // BLOCK

    flat = base * count + mine
    devices = regions * count
    near_tiles = [
        ((flat + devices - 1 + slot // tiles) % devices) * tiles + slot % tiles
        for slot in range(3 * tiles)
    ]

    def share(p, b, slot):
        listed = own_list[0, p, b : b + 1, :]
        live = lax.broadcasted_iota(jnp.int32, listed.shape, 1) < own_counts[0, p : p + 1, b : b + 1]
        hits = live & (listed == near_tiles[slot])
        return jnp.sum(hits.astype(jnp.float32), axis=1, keepdims=True)

    def exchange(p):
        picked = pick(p, ens_ref[...]) if p else tiles_ref[0, 1, 0:members, :]
        center = jnp.mean(picked, axis=0, keepdims=True)
        values = jnp.concatenate([own_values[0, p, t : t + 1, :] for t in range(tiles)], axis=1)
        weights = jnp.concatenate([own_weights[0, p, t : t + 1, :] for t in range(tiles)], axis=1)
        root_weight = jnp.sqrt(weights)
        tiles_ref[p, 1, 0:members, :] = (picked - center) * root_weight
        tiles_ref[p, 1, members : members + 8, :] = jnp.broadcast_to(
            (values - center) * root_weight, (8, values.shape[1])
        )
        copies = [
            remote(
                tiles_ref.at[p, 1], tiles_ref.at[p, 0], tile_send.at[p, 0], tile_recv.at[p, 0], nxt
            ),
            remote(
                tiles_ref.at[p, 1], tiles_ref.at[p, 2], tile_send.at[p, 1], tile_recv.at[p, 1], prv
            ),
        ]
        for copy in copies:
            copy.start()
        return copies

    def gather_systems(p, copies):
        grams = [(members - 1.0) * identity for _ in range(blocks)]
        pulls = [jnp.zeros((members, 1), jnp.float32) for _ in range(blocks)]
        for owner in (1, 0, 2):
            if owner == 0:
                for copy in copies:
                    copy.wait()
            for t in range(tiles):
                lanes = slice(t * LANES, (t + 1) * LANES)
                spread = tiles_ref[p, owner, 0:members, lanes]
                innovation = tiles_ref[p, owner, members : members + 1, lanes]
                halves = split(spread)
                gram = dot3(halves, halves, ((1,), (1,)))
                pull = jnp.sum(spread * innovation, axis=1, keepdims=True)
                slot = owner * tiles + t
                for b in range(blocks):
                    weight = share(p, b, slot)
                    grams[b] = grams[b] + weight * gram
                    pulls[b] = pulls[b] + weight * pull
        return grams, pulls

    def apply(inv_root, pull, b):
        inner = jnp.sum(inv_root * pull, axis=0, keepdims=True)
        shift = jnp.sum(inv_root * inner, axis=1, keepdims=True)
        state = ens_ref[:, b * BLOCK : (b + 1) * BLOCK]
        center = jnp.mean(state, axis=0, keepdims=True)
        anomaly = state - center
        base = center + jnp.sum(shift * anomaly, axis=0, keepdims=True)
        scaled = split(math.sqrt(members - 1) * inv_root)
        return base + dot3(scaled, split(anomaly))

    for p in range(PASSES - 1):
        grams, pulls = gather_systems(p, exchange(p))
        inv_roots = roots(grams, identity)
        for b in range(blocks):
            ens_ref[:, b * BLOCK : (b + 1) * BLOCK] = apply(inv_roots[b], pulls[b], b)

    here = pl.multiple_of(position * window, LANES)

    def out_copy(b, target):
        return remote(
            upd_ref.at[
                pl.ds(pl.multiple_of(target * rows, 8), rows), b * BLOCK : (b + 1) * BLOCK
            ],
            out_ref.at[:, pl.ds(here + b * BLOCK, BLOCK)],
            out_send.at[b, target],
            out_recv.at[b, position],
            (source_region, target),
        )

    def out_own(b):
        return pltpu.make_async_copy(
            upd_ref.at[my_rows, b * BLOCK : (b + 1) * BLOCK],
            out_ref.at[:, pl.ds(here + b * BLOCK, BLOCK)],
            local_sem.at[2 + b],
        )

    def each_target(b, remote_step, local_step):
        def go(k, carry):
            target = (me + count // 2 + k) % count
            stays = (target == me) & (source_region == region)

            @pl.when(jnp.logical_not(stays))
            def _():
                remote_step(out_copy(b, target))

            @pl.when(stays)
            def _():
                local_step(out_own(b))

            return carry

        lax.fori_loop(0, count, go, 0)

    p = PASSES - 1
    grams, pulls = gather_systems(p, exchange(p))
    for b in range(blocks):
        (inv_root,) = roots([grams[b]], identity)
        upd_ref[:, b * BLOCK : (b + 1) * BLOCK] = apply(inv_root, pulls[b], b)
        each_target(b, lambda copy: copy.start(), lambda copy: copy.start())

    lax.fori_loop(0, count, sent_in, 0)
    for b in range(blocks):
        each_target(b, lambda copy: copy.wait_send(), lambda copy: copy.wait())

        def landed(w, carry):
            @pl.when(offset + w != mine)
            def _():
                remote(
                    upd_ref.at[0:rows, b * BLOCK : (b + 1) * BLOCK],
                    out_ref.at[
                        :, pl.ds(pl.multiple_of(w * window + b * BLOCK, LANES), BLOCK)
                    ],
                    out_send.at[b, 0],
                    out_recv.at[b, w],
                    host(offset + w),
                ).wait_recv()

            return carry

        lax.fori_loop(0, count, landed, 0)


def split_rest(value):
    high = value.astype(jnp.bfloat16)
    return high, value - high.astype(jnp.float32)


def local(
    initial_ensemble,
    driving_term,
    observation_cells,
    observation_values,
    observation_weight,
    block_tile_list,
    block_tile_count,
):
    count = lax.axis_size("member")
    regions = lax.axis_size("region")
    tiles_here = observation_cells.shape[2]
    rows, cells = initial_ensemble.shape
    members = rows * count
    window = cells // count
    blocks = window // BLOCK
    kept = pl.BlockSpec(memory_space=pl.ANY)
    wide = cells + 2 * LANES
    f32 = jnp.float32
    dma = pltpu.SemaphoreType.DMA
    return pl.pallas_call(
        functools.partial(kernel, count, regions),
        out_shape=jax.ShapeDtypeStruct((rows, cells), f32),
        in_specs=[kept] * 7,
        out_specs=kept,
        scratch_shapes=[
            pltpu.VMEM((rows, wide), f32),
            pltpu.VMEM((rows, cells), f32),
            pltpu.VMEM((members, window), f32),
            pltpu.VMEM((members, window), f32),
            pltpu.VMEM((1, wide), f32),
            pltpu.VMEM(observation_cells.shape, jnp.int32),
            pltpu.VMEM(observation_values.shape, f32),
            pltpu.VMEM(observation_weight.shape, f32),
            pltpu.VMEM(block_tile_list.shape, jnp.int32),
            pltpu.VMEM(block_tile_count.shape, jnp.int32),
            pltpu.VMEM((PASSES, 3, members + 8, tiles_here * LANES), f32),
            pltpu.VMEM((PASSES, window, tiles_here * LANES), jnp.bfloat16),
            dma((count,)),
            dma((4,)),
            dma((4,)),
            dma((5,)),
            dma((5,)),
            dma((count,)),
            dma((count,)),
            dma((PASSES, 2)),
            dma((PASSES, 2)),
            dma((blocks, count)),
            dma((blocks, count)),
            dma((2 + blocks,)),
        ],
        compiler_params=pltpu.CompilerParams(
            collective_id=0, has_side_effects=True, vmem_limit_bytes=67_043_328
        ),
    )(
        initial_ensemble,
        driving_term[None],
        observation_cells,
        observation_values,
        observation_weight,
        block_tile_list,
        block_tile_count,
    )


def solution(mesh):
    in_specs = (
        P("member", "region"),
        P("region"),
        P(None, None, ("region", "member"), None),
        P(None, None, ("region", "member"), None),
        P(None, None, ("region", "member"), None),
        P(None, None, ("region", "member"), None),
        P(None, None, ("region", "member")),
    )
    out_specs = P("member", "region")
    return jax.shard_map(local, mesh=mesh, in_specs=in_specs, out_specs=out_specs, check_vma=False)
```

```python
import functools
import math

import jax
import jax.numpy as jnp
from jax import lax
from jax.experimental import pallas as pl
from jax.experimental.pallas import tpu as pltpu
from jax.sharding import PartitionSpec as P

BLOCK = 512
NS_ITERS = 10
STEPS = 4
PASSES = 2
LANES = 128
MESH = pl.DeviceIdType.MESH

time_step = 0.05


def split(value):
    high = value.astype(jnp.bfloat16)
    low = (value - high.astype(jnp.float32)).astype(jnp.bfloat16)
    return high, low


def dot3(left, right, contract=((1,), (0,))):
    wide = jnp.concatenate([left[0], left[0], left[1]], axis=contract[0][0])
    deep = jnp.concatenate([right[0], right[1], right[0]], axis=contract[1][0])
    return lax.dot_general(wide, deep, (contract, ((), ())), preferred_element_type=jnp.float32)


def roots(systems, identity):
    frobs = [jnp.sqrt(jnp.sum(s * s, keepdims=True)) for s in systems]
    firsts = [s * (1.0 / f) for s, f in zip(systems, frobs)]

    def quartic(error):
        halves = split(error)
        square = dot3(halves, halves)
        rest = 0.375 * identity + 0.3125 * error + 0.0625 * square
        return 0.5 * error + dot3(split(square), split(rest))

    def close(inv, root):
        return identity - dot3(split(inv), split(root))

    invs, rts, errors = [], [], []
    for first in firsts:
        q = quartic(identity - first)
        invs.append(identity + q)
        rts.append(first + dot3(split(first), split(q)))
    errors = [close(i, r) for i, r in zip(invs, rts)]
    count = len(systems)

    def step(_, state):
        invs, rts, errors = state
        qs = [split(quartic(e)) for e in errors]
        invs = [i + dot3(split(i), q) for i, q in zip(invs, qs)]
        rts = [r + dot3(split(r), q) for r, q in zip(rts, qs)]
        return invs, rts, [close(i, r) for i, r in zip(invs, rts)]

    invs, rts, errors = lax.fori_loop(
        0, NS_ITERS // 2 - 2, step, (invs, rts, errors), unroll=True
    )
    qs = [split(quartic(e)) for e in errors]
    invs = [i + dot3(split(i), q) for i, q in zip(invs, qs)]
    return [i * (1.0 / jnp.sqrt(f)) for i, f in zip(invs, frobs)]


def snake_member(position, count):
    half = count // 2
    late = position // half
    return 2 * position * (1 - late) + (2 * (count - 1 - position) + 1) * late


def snake_position(member, count):
    odd = member % 2
    return (member // 2) * (1 - odd) + (count - 1 - member // 2) * odd


def forecast_window(wide, forcing):
    width = wide.shape[1]
    for _ in range(STEPS):
        ahead_one = pltpu.roll(wide, width - 1, 1)
        behind = pltpu.roll(wide, 1, 1)
        further = pltpu.roll(wide, 2, 1)
        wide = wide + time_step * ((ahead_one - further) * behind - wide + forcing)
    return wide[:, LANES : width - LANES]


def kernel(
    count,
    regions,
    x_ref,
    drive_ref,
    cells_ref,
    values_ref,
    weights_ref,
    list_ref,
    counts_ref,
    out_ref,
    held_ref,
    fc_ref,
    ens_ref,
    upd_ref,
    dheld_ref,
    own_cells,
    own_values,
    own_weights,
    own_list,
    own_counts,
    tiles_ref,
    chosen_ref,
    load_sem,
    halo_send,
    halo_recv,
    obs_send,
    obs_recv,
    in_send,
    in_recv,
    tile_send,
    tile_recv,
    out_send,
    out_recv,
    local_sem,
):
    region = lax.axis_index("region")
    me = lax.axis_index("member")
    rows = fc_ref.shape[0]
    cells = fc_ref.shape[1]
    members = ens_ref.shape[0]
    window = ens_ref.shape[1]
    up = (region + 1) % regions
    down = (region + regions - 1) % regions
    base = region - region % 2
    across = 2 * count
    mine = 2 * snake_position(me, count) + region % 2
    source_region = base + mine // count
    position = mine % count
    offset = (region % 2) * count

    def host(place):
        return (base + place % 2, snake_member(place // 2, count))

    nxt_place = (mine + 1) % across
    nxt = (
        (base + 2 * ((mine + 1) // across) + nxt_place % 2) % regions,
        snake_member(nxt_place // 2, count),
    )
    prv_place = (mine + across - 1) % across
    prv = (
        (base + regions - 2 * ((across - mine) // across) + prv_place % 2) % regions,
        snake_member(prv_place // 2, count),
    )

    def load(w):
        span = pl.ds(pl.multiple_of(w * window, LANES), window)
        kept = pl.ds(pl.multiple_of(w * window + LANES, LANES), window)
        return pltpu.make_async_copy(x_ref.at[:, span], held_ref.at[:, kept], load_sem.at[w])

    def load_all(w, carry):
        load(w).start()
        return carry

    drive_load = pltpu.make_async_copy(
        drive_ref, dheld_ref.at[:, LANES : LANES + cells], local_sem.at[0]
    )
    drive_load.start()
    lax.fori_loop(0, count, load_all, 0)

    barrier = pltpu.get_barrier_semaphore()

    def greet(target):
        pl.semaphore_signal(barrier, inc=1, device_id=target, device_id_type=MESH)

    for k in range(count):
        greet((base + 1 - region % 2, (me + k) % count))
        if k:
            greet((region, (me + k) % count))
    for target in ((up, me), (down, me), nxt, prv):
        greet(target)
    pl.semaphore_wait(barrier, across + 3)

    def remote(source, target, send, recv, device):
        return pltpu.make_async_remote_copy(
            src_ref=source,
            dst_ref=target,
            send_sem=send,
            recv_sem=recv,
            device_id=device,
            device_id_type=MESH,
        )

    last = slice(cells - LANES, cells)
    end = LANES + cells
    halos = [
        remote(
            x_ref.at[:, last], held_ref.at[:, 0:LANES], halo_send.at[0], halo_recv.at[0], (up, me)
        ),
        remote(
            x_ref.at[:, 0:LANES],
            held_ref.at[:, end : end + LANES],
            halo_send.at[1],
            halo_recv.at[1],
            (down, me),
        ),
        remote(
            drive_ref.at[:, last],
            dheld_ref.at[:, 0:LANES],
            halo_send.at[2],
            halo_recv.at[2],
            (up, me),
        ),
        remote(
            drive_ref.at[:, 0:LANES],
            dheld_ref.at[:, end : end + LANES],
            halo_send.at[3],
            halo_recv.at[3],
            (down, me),
        ),
    ]
    for copy in halos:
        copy.start()

    obs_stays = (offset + me) == mine
    obs_pairs = (
        (cells_ref, own_cells),
        (values_ref, own_values),
        (weights_ref, own_weights),
        (list_ref, own_list),
        (counts_ref, own_counts),
    )
    obs_copies = [
        remote(source, target, obs_send.at[i], obs_recv.at[i], host(offset + me))
        for i, (source, target) in enumerate(obs_pairs)
    ]
    obs_locals = [
        pltpu.make_async_copy(source, target, obs_send.at[i])
        for i, (source, target) in enumerate(obs_pairs)
    ]

    @pl.when(jnp.logical_not(obs_stays))
    def _():
        for copy in obs_copies:
            copy.start()

    @pl.when(obs_stays)
    def _():
        for copy in obs_locals:
            copy.start()

    my_rows = pl.ds(pl.multiple_of(me * rows, 8), rows)

    def in_copy(w):
        return remote(
            fc_ref.at[:, pl.ds(pl.multiple_of(w * window, LANES), window)],
            ens_ref.at[my_rows, :],
            in_send.at[w],
            in_recv.at[me],
            host(offset + w),
        )

    def own_window():
        return pltpu.make_async_copy(
            fc_ref.at[:, pl.ds(pl.multiple_of(position * window, LANES), window)],
            ens_ref.at[my_rows, :],
            local_sem.at[1],
        )

    def ship(w):
        @pl.when(offset + w != mine)
        def _():
            in_copy(w).start()

        @pl.when(offset + w == mine)
        def _():
            own_window().start()

    def forecast_at(w):
        wide = pl.ds(pl.multiple_of(w * window, LANES), window + 2 * LANES)
        fc_ref[:, pl.ds(pl.multiple_of(w * window, LANES), window)] = forecast_window(
            held_ref[:, wide], dheld_ref[:, wide]
        )
        ship(w)

    def loaded(w, carry):
        load(w).wait()
        return carry

    def interior(k, carry):
        forecast_at(1 + (first + k) % (count - 2))
        return carry

    quarter = max(count // 4, 1)
    near = snake_position(me, count)
    outer = ((near + quarter) // (2 * quarter)) % 2
    first = (count // 2 - 1) * ((outer + region + 1) % 2)
    drive_load.wait()
    lax.fori_loop(0, count, loaded, 0)
    lax.fori_loop(0, count - 2, interior, 0)
    for copy in halos:
        copy.wait()
    forecast_at(0)
    forecast_at(count - 1)

    @pl.when(jnp.logical_not(obs_stays))
    def _():
        for copy in obs_copies:
            copy.wait()

    @pl.when(obs_stays)
    def _():
        for copy in obs_locals:
            copy.wait()

    tiles = tiles_ref.shape[3] // LANES
    place = lax.broadcasted_iota(jnp.int32, (window, LANES), 0)
    for p in range(PASSES):
        for t in range(tiles):
            hit = place == own_cells[0, p, t : t + 1, :]
            chosen_ref[p, :, t * LANES : (t + 1) * LANES] = hit.astype(jnp.bfloat16)

    def pick(p, state):
        high, rest = split_rest(state)
        middle, rest = split_rest(rest)
        low = rest.astype(jnp.bfloat16)
        terms = jnp.concatenate([high, middle, low], axis=0)
        found = jnp.dot(terms, chosen_ref[p], preferred_element_type=jnp.float32)
        n = state.shape[0]
        return found[:n] + (found[n : 2 * n] + found[2 * n :])

    def arrived(k, carry):
        sender = (me + k) % count
        theirs = pl.ds(pl.multiple_of(sender * rows, 8), rows)
        local_rows = (sender == me) & (source_region == region)

        @pl.when(jnp.logical_not(local_rows))
        def _():
            remote(
                fc_ref.at[:, 0:window],
                ens_ref.at[theirs, :],
                in_send.at[0],
                in_recv.at[sender],
                (source_region, sender),
            ).wait_recv()

        @pl.when(local_rows)
        def _():
            own_window().wait()

        tiles_ref[0, 1, theirs, :] = pick(0, ens_ref[theirs, :])
        return carry

    def sent_in(w, carry):
        @pl.when(offset + w != mine)
        def _():
            in_copy(w).wait_send()

        return carry

    lax.fori_loop(0, count, arrived, 0)

    eye_rows = lax.broadcasted_iota(jnp.int32, (members, members), 0)
    eye_columns = lax.broadcasted_iota(jnp.int32, (members, members), 1)
    identity = (eye_rows == eye_columns).astype(jnp.float32)
    blocks = window // BLOCK

    flat = base * count + mine
    devices = regions * count
    near_tiles = [
        ((flat + devices - 1 + slot // tiles) % devices) * tiles + slot % tiles
        for slot in range(3 * tiles)
    ]

    def share(p, b, slot):
        listed = own_list[0, p, b : b + 1, :]
        live = lax.broadcasted_iota(jnp.int32, listed.shape, 1) < own_counts[0, p : p + 1, b : b + 1]
        hits = live & (listed == near_tiles[slot])
        return jnp.sum(hits.astype(jnp.float32), axis=1, keepdims=True)

    def exchange(p):
        picked = pick(p, ens_ref[...]) if p else tiles_ref[0, 1, 0:members, :]
        center = jnp.mean(picked, axis=0, keepdims=True)
        values = jnp.concatenate([own_values[0, p, t : t + 1, :] for t in range(tiles)], axis=1)
        weights = jnp.concatenate([own_weights[0, p, t : t + 1, :] for t in range(tiles)], axis=1)
        root_weight = jnp.sqrt(weights)
        tiles_ref[p, 1, 0:members, :] = (picked - center) * root_weight
        tiles_ref[p, 1, members : members + 8, :] = jnp.broadcast_to(
            (values - center) * root_weight, (8, values.shape[1])
        )
        copies = [
            remote(
                tiles_ref.at[p, 1], tiles_ref.at[p, 0], tile_send.at[p, 0], tile_recv.at[p, 0], nxt
            ),
            remote(
                tiles_ref.at[p, 1], tiles_ref.at[p, 2], tile_send.at[p, 1], tile_recv.at[p, 1], prv
            ),
        ]
        for copy in copies:
            copy.start()
        return copies

    def gather_systems(p, copies):
        grams = [(members - 1.0) * identity for _ in range(blocks)]
        pulls = [jnp.zeros((members, 1), jnp.float32) for _ in range(blocks)]
        for owner in (1, 0, 2):
            if owner != 1:
                copies[owner // 2].wait()
            for t in range(tiles):
                lanes = slice(t * LANES, (t + 1) * LANES)
                spread = tiles_ref[p, owner, 0:members, lanes]
                innovation = tiles_ref[p, owner, members : members + 1, lanes]
                halves = split(spread)
                gram = dot3(halves, halves, ((1,), (1,)))
                pull = jnp.sum(spread * innovation, axis=1, keepdims=True)
                slot = owner * tiles + t
                for b in range(blocks):
                    weight = share(p, b, slot)
                    grams[b] = grams[b] + weight * gram
                    pulls[b] = pulls[b] + weight * pull
        return grams, pulls

    def apply(inv_root, pull, b):
        inner = jnp.sum(inv_root * pull, axis=0, keepdims=True)
        shift = jnp.sum(inv_root * inner, axis=1, keepdims=True)
        state = ens_ref[:, b * BLOCK : (b + 1) * BLOCK]
        center = jnp.mean(state, axis=0, keepdims=True)
        anomaly = state - center
        base = center + jnp.sum(shift * anomaly, axis=0, keepdims=True)
        scaled = split(math.sqrt(members - 1) * inv_root)
        return base + dot3(scaled, split(anomaly))

    for p in range(PASSES - 1):
        grams, pulls = gather_systems(p, exchange(p))
        inv_roots = roots(grams, identity)
        for b in range(blocks):
            ens_ref[:, b * BLOCK : (b + 1) * BLOCK] = apply(inv_roots[b], pulls[b], b)

    here = pl.multiple_of(position * window, LANES)

    def out_copy(b, target):
        return remote(
            upd_ref.at[
                pl.ds(pl.multiple_of(target * rows, 8), rows), b * BLOCK : (b + 1) * BLOCK
            ],
            out_ref.at[:, pl.ds(here + b * BLOCK, BLOCK)],
            out_send.at[b, target],
            out_recv.at[b, position],
            (source_region, target),
        )

    def out_own(b):
        return pltpu.make_async_copy(
            upd_ref.at[my_rows, b * BLOCK : (b + 1) * BLOCK],
            out_ref.at[:, pl.ds(here + b * BLOCK, BLOCK)],
            local_sem.at[2 + b],
        )

    def each_target(b, remote_step, local_step):
        def go(k, carry):
            target = (me + count // 2 + k) % count
            stays = (target == me) & (source_region == region)

            @pl.when(jnp.logical_not(stays))
            def _():
                remote_step(out_copy(b, target))

            @pl.when(stays)
            def _():
                local_step(out_own(b))

            return carry

        lax.fori_loop(0, count, go, 0)

    p = PASSES - 1
    grams, pulls = gather_systems(p, exchange(p))
    for b in range(blocks):
        (inv_root,) = roots([grams[b]], identity)
        upd_ref[:, b * BLOCK : (b + 1) * BLOCK] = apply(inv_root, pulls[b], b)
        each_target(b, lambda copy: copy.start(), lambda copy: copy.start())

    lax.fori_loop(0, count, sent_in, 0)
    for b in range(blocks):
        each_target(b, lambda copy: copy.wait_send(), lambda copy: copy.wait())

        def landed(w, carry):
            @pl.when(offset + w != mine)
            def _():
                remote(
                    upd_ref.at[0:rows, b * BLOCK : (b + 1) * BLOCK],
                    out_ref.at[
                        :, pl.ds(pl.multiple_of(w * window + b * BLOCK, LANES), BLOCK)
                    ],
                    out_send.at[b, 0],
                    out_recv.at[b, w],
                    host(offset + w),
                ).wait_recv()

            return carry

        lax.fori_loop(0, count, landed, 0)


def split_rest(value):
    high = value.astype(jnp.bfloat16)
    return high, value - high.astype(jnp.float32)


def local(
    initial_ensemble,
    driving_term,
    observation_cells,
    observation_values,
    observation_weight,
    block_tile_list,
    block_tile_count,
):
    count = lax.axis_size("member")
    regions = lax.axis_size("region")
    tiles_here = observation_cells.shape[2]
    rows, cells = initial_ensemble.shape
    members = rows * count
    window = cells // count
    blocks = window // BLOCK
    kept = pl.BlockSpec(memory_space=pl.ANY)
    wide = cells + 2 * LANES
    f32 = jnp.float32
    dma = pltpu.SemaphoreType.DMA
    return pl.pallas_call(
        functools.partial(kernel, count, regions),
        out_shape=jax.ShapeDtypeStruct((rows, cells), f32),
        in_specs=[kept] * 7,
        out_specs=kept,
        scratch_shapes=[
            pltpu.VMEM((rows, wide), f32),
            pltpu.VMEM((rows, cells), f32),
            pltpu.VMEM((members, window), f32),
            pltpu.VMEM((members, window), f32),
            pltpu.VMEM((1, wide), f32),
            pltpu.VMEM(observation_cells.shape, jnp.int32),
            pltpu.VMEM(observation_values.shape, f32),
            pltpu.VMEM(observation_weight.shape, f32),
            pltpu.VMEM(block_tile_list.shape, jnp.int32),
            pltpu.VMEM(block_tile_count.shape, jnp.int32),
            pltpu.VMEM((PASSES, 3, members + 8, tiles_here * LANES), f32),
            pltpu.VMEM((PASSES, window, tiles_here * LANES), jnp.bfloat16),
            dma((count,)),
            dma((4,)),
            dma((4,)),
            dma((5,)),
            dma((5,)),
            dma((count,)),
            dma((count,)),
            dma((PASSES, 2)),
            dma((PASSES, 2)),
            dma((blocks, count)),
            dma((blocks, count)),
            dma((2 + blocks,)),
        ],
        compiler_params=pltpu.CompilerParams(
            collective_id=0, has_side_effects=True, vmem_limit_bytes=67_043_328
        ),
    )(
        initial_ensemble,
        driving_term[None],
        observation_cells,
        observation_values,
        observation_weight,
        block_tile_list,
        block_tile_count,
    )


def solution(mesh):
    in_specs = (
        P("member", "region"),
        P("region"),
        P(None, None, ("region", "member"), None),
        P(None, None, ("region", "member"), None),
        P(None, None, ("region", "member"), None),
        P(None, None, ("region", "member"), None),
        P(None, None, ("region", "member")),
    )
    out_specs = P("member", "region")
    return jax.shard_map(local, mesh=mesh, in_specs=in_specs, out_specs=out_specs, check_vma=False)
```
